512 devices in a mesh: dp: 32 (over x, z), tensor: 16 (over y, core).
Axes of the slice: x: 4, y: 8, z: 8, core: 2. Of those that a mesh axis runs over, the one named last changes fastest.
Arguments:
- tokens: bfloat16 [512, 3072], P('dp'), may hold values from -6 to 6
- cotangent: bfloat16 [512, 3072], P('dp'), may hold values from -6 to 6
- routes: int32 [512, 2], P('dp'), may hold values from 0 to 7, all different within a row; in each aligned block of 16 rows (0 to 15, 16 to 31, ...) at most 8 rows name the same one
- gates: float32 [512, 2], P('dp'), may hold values from 0.2 to 1
- w_gate: bfloat16 [3072, 131072], P(None, ('dp', 'tensor')), may hold values from -0.109375 to 0.109375
- w_up: bfloat16 [3072, 131072], P(None, ('dp', 'tensor')), may hold values from -0.109375 to 0.109375
- w_down: bfloat16 [131072, 3072], P('dp', 'tensor'), may hold values from -0.046875 to 0.046875
Outputs:
- mixed_out: bfloat16 [512, 3072], P('dp', 'tensor')
- d_tokens: bfloat16 [512, 3072], P('dp', 'tensor')
The draws below stay inside these ranges and needn't reach their ends.
Inputs may be any that keep to these rules, and one draw needn't show every extreme that they name: `routes`: among the tokens of one index of dp (aligned blocks of 16 rows) no expert is chosen more than 8 times, and some expert is chosen exactly 8 times; the 2 experts of a token differ.
All inputs are finite; a program needn't handle non-finite values.
Results may differ from the reference program's by a relative error of at most 0.0057.
Values may be sent and summed in bfloat16 or wider, within the bound.
No kernel may reach another device: no remote copies, remote signals or barrier semaphores. Data moves between devices by JAX's collectives and lax.ppermute only.
A program may use at most 64 MiB of HBM per device.

```python
import math
import jax
import jax.numpy as jnp
import numpy as np
from jax import lax

D = 3072
EXPERTS = 8
TOP = 2
TOK_DEV = 16
FF = 16384
CAP = 8
TOKENS = 512
N_DP = 32


def block_scale(own_key, dims, split, low, top_value):
    loudness, own = 1.0, jax.random.fold_in(own_key, 6)
    for position, shards_of in split:
        heights = jnp.exp(jax.random.uniform(jax.random.fold_in(own, position), (shards_of,), jnp.float32, low / len(split), top_value / len(split)))
        loudness = loudness * jnp.repeat(heights, dims[position] // shards_of).reshape([-1 if axis == position else 1 for axis in range(len(dims))])
    return loudness


def shared_out(rng, own, number, rows, amount, top, most, skew):
    sequence = jax.random.permutation(rng, amount)
    crowded, ordinary = shares(amount, rows * top, most, skew, True), shares(amount, rows * top, most, skew, False)
    places = jnp.arange(amount)

    def named(tallies, offset_by):
        used = int((tallies > 0).sum())
        fixed = max(1, used // 4)
        passed = fixed + (places - fixed + offset_by * (used - fixed)) % max(1, amount - fixed)
        return jnp.zeros((amount,), jnp.int32).at[sequence[jnp.where(places < fixed, places, passed)]].set(jnp.asarray(tallies, jnp.int32))

    tallies = jnp.where(number % 4 == 0, named(crowded, number // 4), named(ordinary, number - number // 4 - 1))
    mixed = jax.random.permutation(jax.random.fold_in(own, 3), amount)
    giver, receiver = mixed[0:amount // 2 * 2:2], mixed[1:amount // 2 * 2:2]
    slack = jnp.minimum(tallies[giver] - 1, most - tallies[receiver]) // 2
    slack = jnp.where((giver == sequence[0]) | (receiver == sequence[0]) | (tallies[receiver] == 0), 0, jnp.maximum(slack, 0))
    passed = jax.random.randint(jax.random.fold_in(own, 4), (amount // 2,), 0, 1 << 20) % (slack + 1)
    tallies = tallies.at[giver].add(-passed).at[receiver].add(passed)
    items = jnp.searchsorted(jnp.cumsum(tallies), jnp.arange(rows * top), side="right").astype(jnp.int32)
    table = items.reshape(top, rows).T
    table = table[jax.random.permutation(jax.random.fold_in(own, 1), rows)]
    offset_by = jax.random.randint(jax.random.fold_in(own, 2), (rows, 1), 0, top)
    return jnp.take_along_axis(table, (jnp.arange(top)[None, :] + offset_by) % top, axis=1)


def shares(number_of, total, most, lean, full):
    loads = [(1 << 20) // math.isqrt(rank ** lean) + 1 for rank in range(1, number_of + 1)]
    largest = most if full else min(most, max(-(-total // number_of), total * loads[0] // sum(loads)))
    least = 1 if total - largest >= number_of - 1 else 0
    given, spare = [largest] + [least] * (number_of - 1), total - largest - least * (number_of - 1)
    while spare > 0:
        candidates = [i for i in range(1, number_of) if given[i] < largest] or [i for i in range(1, number_of) if given[i] < most]
        whole, remaining = sum([loads[i] for i in candidates]), spare
        for i in candidates:
            more = min(most - given[i], max(1, remaining * loads[i] // whole), spare)
            given[i] = given[i] + more
            spare = spare - more
    return np.array(given)


def noise(stream_key, dims, scale, bound, cuts=(), kind=jnp.bfloat16):
    gain = block_scale(stream_key, dims, cuts, -0.22, 0.18) if cuts else 1.0
    entries = jax.random.normal(stream_key, dims, jnp.float32) * scale * gain
    return jnp.minimum(jnp.maximum(entries, -bound), bound).astype(kind)


def setup_inputs(seed: int = 0) -> dict:
    key_list = jax.random.split(jax.random.key(seed), 8)
    tokens = noise(key_list[0], (TOKENS, D), 1.0, 6.0, ((0, 32),))
    cotangent = noise(key_list[1], (TOKENS, D), 1.0, 6.0, ((0, 32),))
    routes_keys = jax.random.split(jax.random.fold_in(key_list[2], 1), TOKENS // TOK_DEV)
    routes_turns = jax.random.permutation(jax.random.fold_in(key_list[2], 3), TOKENS // TOK_DEV)
    routes = jax.vmap(lambda own, number: shared_out(jax.random.fold_in(key_list[2], 2), own, number, TOK_DEV, EXPERTS, TOP, CAP, 2))(routes_keys, routes_turns).reshape((TOKENS, TOP))
    gates = jnp.clip(0.2 + 0.8 * jax.random.uniform(key_list[3], (TOKENS, TOP), jnp.float32) ** block_scale(key_list[3], (TOKENS, TOP), ((0, 32),), -0.2, 0.2), 0.2, 1.0)
    w_gate = noise(key_list[4], (D, EXPERTS * FF), D ** -0.5, 0.109375, ((1, 512),))
    w_up = noise(key_list[5], (D, EXPERTS * FF), D ** -0.5, 0.109375, ((1, 512),))
    w_down = noise(key_list[6], (EXPERTS * FF, D), FF ** -0.5, 0.046875, ((0, 32), (1, 16)))
    return {"tokens": tokens, "cotangent": cotangent, "routes": routes, "gates": gates, "w_gate": w_gate, "w_up": w_up, "w_down": w_down}


def reference(tokens, cotangent, routes, gates, w_gate, w_up, w_down):
    top_k = routes.shape[1]
    model_width = tokens.shape[1]
    flat_routes = routes.reshape(-1).astype(jnp.int32)
    assigned = flat_routes.shape[0]
    x_rows = jnp.repeat(tokens, top_k, axis=0)
    dy_rows = (jnp.repeat(cotangent.astype(jnp.float32), top_k, axis=0) * gates.reshape(-1)[:, None]).astype(jnp.bfloat16)
    zero_row = jnp.zeros((1, model_width), jnp.bfloat16)
    x_padded = jnp.concatenate([x_rows, zero_row], axis=0)
    dy_padded = jnp.concatenate([dy_rows, zero_row], axis=0)
    gate_experts = w_gate.reshape(model_width, EXPERTS, FF)
    up_experts = w_up.reshape(model_width, EXPERTS, FF)
    down_experts = w_down.reshape(EXPERTS, FF, model_width)
    limit = N_DP * CAP

    def expert_pass(expert):
        index = jnp.nonzero(flat_routes == expert, size=limit, fill_value=assigned)[0].astype(jnp.int32)
        x_in = x_padded[index]
        dy_in = dy_padded[index]
        gate_mat = lax.dynamic_index_in_dim(gate_experts, expert, 1, keepdims=False)
        up_mat = lax.dynamic_index_in_dim(up_experts, expert, 1, keepdims=False)
        down_mat = lax.dynamic_index_in_dim(down_experts, expert, 0, keepdims=False)
        gate_pre = jnp.dot(x_in, gate_mat, preferred_element_type=jnp.float32)
        up_pre = jnp.dot(x_in, up_mat, preferred_element_type=jnp.float32)
        sigmoid_gate = jax.nn.sigmoid(gate_pre)
        activated = gate_pre * sigmoid_gate
        hidden = (activated * up_pre).astype(jnp.bfloat16)
        out_rows = jnp.dot(hidden, down_mat, preferred_element_type=jnp.float32)
        d_hidden = jnp.dot(dy_in, down_mat.T, preferred_element_type=jnp.float32)
        d_gate = (d_hidden * up_pre * sigmoid_gate * (1.0 + gate_pre * (1.0 - sigmoid_gate))).astype(jnp.bfloat16)
        d_up = (d_hidden * activated).astype(jnp.bfloat16)
        grad_rows = jnp.dot(d_gate, gate_mat.T, preferred_element_type=jnp.float32) + jnp.dot(d_up, up_mat.T, preferred_element_type=jnp.float32)
        return index, out_rows, grad_rows

    index, out_rows, grad_rows = lax.map(expert_pass, jnp.arange(EXPERTS, dtype=jnp.int32))
    flat_index = index.reshape(-1)
    out_all = jnp.zeros((assigned + 1, model_width), jnp.float32).at[flat_index].add(out_rows.reshape(-1, model_width))[:assigned]
    grad_all = jnp.zeros((assigned + 1, model_width), jnp.float32).at[flat_index].add(grad_rows.reshape(-1, model_width))[:assigned]
    mixed_out = jnp.sum(out_all.reshape(-1, top_k, model_width) * gates[:, :, None], axis=1).astype(jnp.bfloat16)
    d_tokens = jnp.sum(grad_all.reshape(-1, top_k, model_width), axis=1).astype(jnp.bfloat16)
    return mixed_out, d_tokens
```

```python
import jax
import jax.numpy as jnp
from jax import lax
from jax.sharding import Mesh, PartitionSpec as P

EXPERTS = 8
CAP = 8
DP = ("x", "z")
SWAP = ((0, 1), (1, 0))


def mm(a, b):
    return jnp.dot(a, b, preferred_element_type=jnp.float32)


def mm_t(a, b):
    return lax.dot_general(a, b, (((1,), (1,)), ((), ())), preferred_element_type=jnp.float32)


def turn_down(w_down, core, row, rows):
    cols = w_down.shape[1]
    width = w_down.shape[0] // (2 * rows)
    down = w_down.T.reshape(cols, rows, 2, width)
    own = lax.dynamic_index_in_dim(down, core, 2, keepdims=False).transpose(1, 0, 2)
    away = lax.dynamic_index_in_dim(down, 1 - core, 2, keepdims=False).transpose(1, 0, 2)
    other = lax.ppermute(away, "c", SWAP)
    both = jnp.stack([own, other], axis=1)
    got = both
    for shift in (1, 7, 2, 6, 3, 5, 4):
        perm = [(i, (i + shift) % rows) for i in range(rows)]
        piece = lax.dynamic_index_in_dim(both, (row + shift) % rows, 0, keepdims=False)
        piece = lax.ppermute(piece, "y", perm)
        got = lax.dynamic_update_index_in_dim(got, piece, (row - shift) % rows, 0)
    return got[:, 0].reshape(rows * cols, width), got[:, 1].reshape(rows * cols, width)


def body(tokens, cotangent, routes, gates, w_gate, w_up, w_down):
    count_tok, model = tokens.shape
    top = routes.shape[1]
    half = model // 2
    n_dp = lax.axis_size(DP)
    rows = lax.axis_size("y")
    copies = n_dp // EXPERTS
    slots = EXPERTS * CAP
    core, row = lax.axis_index("c"), lax.axis_index("y")
    cols = w_down.shape[1]

    down_own, down_other = turn_down(w_down, core, row, rows)

    flat = routes.reshape(-1)
    order = jnp.arange(flat.shape[0], dtype=jnp.int32)
    earlier = (flat[:, None] == flat[None, :]) & (order[None, :] < order[:, None])
    target = flat * CAP + jnp.sum(earlier.astype(jnp.int32), axis=1)
    placing = jnp.arange(slots, dtype=jnp.int32)[:, None] == target[None, :]
    slot_gate = jnp.sum(jnp.where(placing, gates.reshape(-1)[None, :], 0.0), axis=1)
    of_token = jnp.any(placing.reshape(slots, count_tok, top), axis=2).astype(jnp.bfloat16)
    x_half = lax.dynamic_slice_in_dim(tokens, core * half, half, 1)
    dy_half = lax.dynamic_index_in_dim(
        cotangent.reshape(count_tok, rows, 2, cols), core, 2, keepdims=False
    ).reshape(count_tok, half)
    x_out = mm(of_token, x_half).astype(jnp.bfloat16)
    dy_out = (mm(of_token, dy_half) * slot_gate[:, None]).astype(jnp.bfloat16)
    packed = jnp.concatenate([x_out, dy_out], axis=1).reshape(EXPERTS, CAP, model)
    sent = jnp.repeat(packed, copies, axis=0)
    got = lax.all_to_all(sent, DP, split_axis=0, concat_axis=0, tiled=True)
    got = got.reshape(n_dp * CAP, model)
    partner = lax.ppermute(got, "c", SWAP)
    x_low = jnp.where(core == 0, got[:, :half], partner[:, :half])
    x_high = jnp.where(core == 0, partner[:, :half], got[:, :half])
    x_in = jnp.concatenate([x_low, x_high], axis=1)

    gate_pre = mm(x_in, w_gate)
    up_pre = mm(x_in, w_up)
    s = jax.nn.sigmoid(gate_pre)
    activated = gate_pre * s
    hidden = (activated * up_pre).astype(jnp.bfloat16)
    d_hidden = mm(got[:, half:], down_own) + mm(partner[:, half:], down_other)
    d_gate = (d_hidden * up_pre * s * (1.0 + gate_pre * (1.0 - s))).astype(jnp.bfloat16)
    d_up = (d_hidden * activated).astype(jnp.bfloat16)

    gate_rows = w_gate.reshape(rows, 2, cols, -1)
    up_rows = w_up.reshape(rows, 2, cols, -1)

    def partial(parity, down):
        g = lax.dynamic_index_in_dim(gate_rows, parity, 1, keepdims=False).reshape(half, -1)
        u = lax.dynamic_index_in_dim(up_rows, parity, 1, keepdims=False).reshape(half, -1)
        out = mm_t(hidden, down).reshape(-1, rows, cols)
        grad = (mm_t(d_gate, g) + mm_t(d_up, u)).reshape(-1, rows, cols)
        return jnp.concatenate([out, grad], axis=2).transpose(1, 0, 2)

    away = partial(1 - core, down_other).astype(jnp.bfloat16)
    near = partial(core, down_own)
    total = (near + lax.ppermute(away, "c", SWAP).astype(jnp.float32)).astype(jnp.bfloat16)
    back = lax.all_to_all(total, "y", split_axis=0, concat_axis=0, tiled=True)
    back = jnp.sum(back.astype(jnp.float32), axis=0).astype(jnp.bfloat16)
    back = back.reshape(n_dp, CAP, 2 * cols)
    back = lax.all_to_all(back, DP, split_axis=0, concat_axis=0, tiled=True)
    back = back.reshape(EXPERTS, copies, CAP, 2 * cols).astype(jnp.float32)
    summed = jnp.sum(back, axis=1).reshape(slots, 2 * cols)

    def unpack(weights, values):
        return lax.dot_general(
            weights,
            values,
            (((0,), (0,)), ((), ())),
            precision=lax.Precision.HIGHEST,
            preferred_element_type=jnp.float32,
        ).astype(jnp.bfloat16)

    weight = jnp.sum(
        jnp.where(placing, gates.reshape(-1)[None, :], 0.0).reshape(slots, count_tok, top), axis=2
    )
    return (
        unpack(weight, summed[:, :cols]),
        unpack(of_token.astype(jnp.float32), summed[:, cols:]),
    )


def solution(mesh):
    size = dict(x=4, z=8, y=8, c=2)
    fine = Mesh(mesh.devices.reshape(tuple(size.values())), tuple(size))
    dp, tensor = DP, ("y", "c")
    placed = (P(dp, None),) * 4 + (P(None, dp + tensor),) * 2 + (P(dp, tensor),)
    return jax.shard_map(
        body,
        mesh=fine,
        in_specs=placed,
        out_specs=(P(dp, tensor), P(dp, tensor)),
        check_vma=False,
    )
```

```python
import jax
import jax.numpy as jnp
from jax import lax
from jax.experimental import pallas as pl
from jax.experimental.pallas import tpu as pltpu
from jax.sharding import Mesh, PartitionSpec as P

EXPERTS = 8
CAP = 8
DP = ("x", "z")
SWAP = ((0, 1), (1, 0))
F32, BF16 = jnp.float32, jnp.bfloat16
VMEM = pl.BlockSpec(memory_space=pltpu.VMEM)
HBM = pl.BlockSpec(memory_space=pltpu.MemorySpace.HBM)
SMEM = pl.BlockSpec(memory_space=pltpu.SMEM)


def params(mib):
    return pltpu.CompilerParams(vmem_limit_bytes=mib * 2**20)


ROWS = 8
SHIFTS = (4, 3, 5, 2, 6, 1, 7)


def pin(a):
    return pltpu.with_memory_space_constraint(a, pltpu.MemorySpace.HBM)


def mm(a, b):
    return jnp.dot(a, b, preferred_element_type=F32)


def mm_t(a, b):
    return lax.dot_general(a, b, (((1,), (1,)), ((), ())), preferred_element_type=F32)


def shape(*dims, dtype=BF16):
    return jax.ShapeDtypeStruct(dims, dtype)


def slot_table(routes, gates, by_token):
    slots = EXPERTS * CAP
    count_tok = routes.shape[0] if by_token else routes.shape[1]
    dims, axis = ((count_tok, slots), 1) if by_token else ((slots, count_tok), 0)
    pick = (lambda a, k: a[:, k : k + 1]) if by_token else (lambda a, k: a[k : k + 1, :])
    slot = lax.broadcasted_iota(jnp.int32, dims, axis)
    first, second = pick(routes, 0) == slot // CAP, pick(routes, 1) == slot // CAP
    member = jnp.where(first | second, 1.0, 0.0).astype(BF16)
    a = lax.broadcasted_iota(jnp.int32, (count_tok, count_tok), axis)
    b = lax.broadcasted_iota(jnp.int32, (count_tok, count_tok), 1 - axis)
    earlier = jnp.where(a < b, 1.0, 0.0).astype(BF16)
    rank = mm(earlier, member) if by_token else mm(member, earlier)
    mine = jnp.where((rank == (slot % CAP).astype(F32)) & (first | second), 1.0, 0.0)
    gate = jnp.where(first, pick(gates, 0), 0.0) + jnp.where(second, pick(gates, 1), 0.0)
    return mine, mine * gate


def first_kernel(at_ref, tokens_hbm, cot_hbm, routes_hbm, gates_hbm, gate_hbm, up_hbm, down_hbm, sent_ref, *rest):
    cut, away_hbm, held, sems = rest[: ROWS - 1], rest[ROWS - 1], rest[ROWS : ROWS + 4], rest[ROWS + 4]
    cols, width = cut[0].shape
    moves = list(zip((tokens_hbm, cot_hbm, routes_hbm, gates_hbm), held))
    for i, source in enumerate((gate_hbm, up_hbm)):
        for y in range(ROWS):
            rows = pl.ds(pl.multiple_of((2 * y + 1 - at_ref[0]) * cols, cols), cols)
            moves.append((source.at[rows], away_hbm.at[i, pl.ds(y * cols, cols)]))
    for shift, to in zip(SHIFTS, cut):
        y = lax.rem(at_ref[1] + shift, ROWS)
        moves.append((down_hbm.at[:, pl.ds(pl.multiple_of(y * width, width), width)], to))
    copies = [pltpu.make_async_copy(*move, sems.at[i]) for i, move in enumerate(moves)]
    for copy in copies:
        copy.start()
    for copy in copies[:4]:
        copy.wait()
    tokens_ref, cot_ref, routes_ref, gates_ref = held
    model = tokens_ref.shape[1]
    half = model // 2
    low = at_ref[0] == 0
    mine, gate = slot_table(routes_ref[...], gates_ref[...], False)
    gate = jnp.sum(gate, axis=1, keepdims=True)
    mine = mine.astype(BF16)

    def ours(ref):
        cut = [ref[:, i * cols : (i + 1) * cols] for i in range(2 * ROWS)]
        return jnp.concatenate([jnp.where(low, cut[2 * y], cut[2 * y + 1]) for y in range(ROWS)], axis=1)

    x = mm(mine, ours(tokens_ref)).reshape(EXPERTS, CAP, half).astype(BF16)
    dy = (mm(mine, ours(cot_ref)) * gate).reshape(EXPERTS, CAP, half).astype(BF16)
    for copy in range(sent_ref.shape[1]):
        sent_ref[:, copy, :, :half] = x
        sent_ref[:, copy, :, half:] = dy
    for copy in copies[4:]:
        copy.wait()


def weight_copies(at_ref, gate_hbm, up_hbm, far_hbm, down_hbm, pieces, gate_w, up_w, down_w, sems):
    cols, width = gate_w.shape[1], gate_w.shape[2] // 2
    steps = []
    for i, shift in enumerate((0, *SHIFTS)):
        y = lax.rem(at_ref[1] - shift + ROWS, ROWS)
        rows = pl.ds(pl.multiple_of((2 * y + at_ref[0]) * cols, cols), cols)
        far = pl.ds(pl.multiple_of(y * cols, cols), cols)
        own_units = pl.ds(pl.multiple_of(at_ref[1] * 2 * width, 2 * width), 2 * width)
        moves = [
            (gate_hbm.at[rows], gate_w.at[y, :, pl.ds(0, width)]),
            (far_hbm.at[0, far], gate_w.at[y, :, pl.ds(width, width)]),
            (up_hbm.at[rows], up_w.at[y, :, pl.ds(0, width)]),
            (far_hbm.at[1, far], up_w.at[y, :, pl.ds(width, width)]),
            (down_hbm.at[:, own_units] if shift == 0 else pieces[i - 1], down_w.at[y]),
        ]
        copies = [pltpu.make_async_copy(*move, sems.at[5 * i + j]) for j, move in enumerate(moves)]
        steps.append((y, copies))
    return steps


def before_kernel(at_ref, got_ref, gate_hbm, up_hbm, far_hbm, down_hbm, *rest):
    pieces, (keep_ref, send_ref, gate_w, up_w, down_w, sems) = rest[: ROWS - 1], rest[ROWS - 1 :]
    steps = weight_copies(at_ref, gate_hbm, up_hbm, far_hbm, down_hbm, pieces, gate_w, up_w, down_w, sems)
    for j in range(5):
        for _, copies in steps:
            copies[j].start()
    low = at_ref[0] == 0
    half = got_ref.shape[1] // 2
    width = keep_ref.shape[2]
    for i, (weight, part, needs) in enumerate(((gate_w, 0, (0, 1)), (up_w, 0, (2, 3)), (down_w, 1, (4,)))):
        for _, copies in steps:
            for j in needs:
                copies[j].wait()
        both = mm(got_ref[:, part * half : (part + 1) * half], weight[...].reshape(half, 2 * width))
        left, right = both[:, :width], both[:, width:]
        if part:
            left, right = jnp.where(low, left, right), jnp.where(low, right, left)
        keep_ref[i] = left
        send_ref[i] = right


def middle_kernel(keep_ref, came_ref, act_ref):
    gate_pre, up_pre, d_hidden = (keep_ref[i] + came_ref[i] for i in range(3))
    s = jax.nn.sigmoid(gate_pre)
    activated = gate_pre * s
    act_ref[0] = (activated * up_pre).astype(BF16)
    act_ref[1] = (d_hidden * up_pre * s * (1.0 + gate_pre * (1.0 - s))).astype(BF16)
    act_ref[2] = (d_hidden * activated).astype(BF16)


def after_kernel(at_ref, act_ref, came_ref, gate_w, up_w, down_w, sent_ref):
    low = at_ref[0] == 0
    block = 2 * gate_w.shape[1]
    hidden = jnp.concatenate(
        [jnp.where(low, act_ref[0], came_ref[0]), jnp.where(low, came_ref[0], act_ref[0])], axis=1
    )
    d_gate = jnp.concatenate([act_ref[1], came_ref[1]], axis=1)
    d_up = jnp.concatenate([act_ref[2], came_ref[2]], axis=1)
    for y in range(ROWS):
        out = mm_t(hidden, down_w[y])
        grad = mm_t(d_gate, gate_w[y]) + mm_t(d_up, up_w[y])
        sent_ref[:, y * block : (y + 1) * block] = jnp.concatenate([out, grad], axis=1).astype(BF16)


def combine_kernel(back_ref, routes_ref, gates_ref, mixed_ref):
    cols = mixed_ref.shape[2] // 2
    summed = back_ref[:, 0].astype(F32)
    for copy in range(1, back_ref.shape[1]):
        summed = summed + back_ref[:, copy].astype(F32)
    summed = summed.reshape(EXPERTS * CAP, -1)
    mine, gate = slot_table(routes_ref[...], gates_ref[...], True)

    def pick(weights, values):
        return jnp.dot(weights, values, precision=lax.Precision.HIGHEST, preferred_element_type=F32)

    for y in range(ROWS):
        out = pick(gate, summed[:, 2 * y * cols : (2 * y + 1) * cols])
        grad = pick(mine, summed[:, (2 * y + 1) * cols : 2 * (y + 1) * cols])
        mixed_ref[y] = jnp.concatenate([out, grad], axis=1).astype(BF16)


def call(kernel, out_shape, *args, scalars=0, mib=8):
    single = not isinstance(out_shape, list)
    return pl.pallas_call(
        kernel,
        in_specs=[SMEM] * scalars + [VMEM] * (len(args) - scalars),
        out_specs=VMEM if single else [VMEM] * len(out_shape),
        out_shape=out_shape,
        compiler_params=params(mib),
    )(*args)


def body(tokens, cotangent, routes, gates, w_gate, w_up, w_down):
    count_tok, model = tokens.shape
    n_dp = lax.axis_size(DP)
    copies = n_dp // EXPERTS
    cols, width = w_down.shape[1], w_gate.shape[1]
    lines, half = n_dp * CAP, model // 2
    at = jnp.stack([lax.axis_index("c"), lax.axis_index("y")]).astype(jnp.int32)
    down = w_down.T

    held = (tokens, cotangent, routes.T, gates.T)
    sent, *cut, away = pl.pallas_call(
        first_kernel,
        in_specs=[SMEM] + [HBM] * 7,
        out_specs=[VMEM] + [HBM] * ROWS,
        out_shape=[shape(EXPERTS, copies, CAP, model)]
        + [shape(cols, 2 * width)] * (ROWS - 1)
        + [shape(2, half, width)],
        scratch_shapes=[pltpu.VMEM(a.shape, a.dtype) for a in held]
        + [pltpu.SemaphoreType.DMA((4 + 2 * ROWS + ROWS - 1,))],
        compiler_params=params(8),
    )(at, *(pin(a) for a in (*held, w_gate, w_up, down)))
    got = lax.all_to_all(sent.reshape(n_dp, CAP, model), DP, split_axis=0, concat_axis=0, tiled=True)

    far = lax.ppermute(away, "c", SWAP)
    *late, far = lax.optimization_barrier((*cut[4:], far))
    cut = tuple(pin(a) for a in (*cut[:4], *late))
    pieces = [lax.ppermute(a, "y", [(i, (i + s) % ROWS) for i in range(ROWS)]) for a, s in zip(cut, SHIFTS)]

    got, *pieces = lax.optimization_barrier((got, *pieces))
    keep, send, *weights = pl.pallas_call(
        before_kernel,
        in_specs=[SMEM, VMEM] + [HBM] * (3 + ROWS),
        out_specs=[VMEM] * 5,
        out_shape=[shape(3, lines, width, dtype=F32)] * 2 + [shape(ROWS, cols, 2 * width)] * 3,
        scratch_shapes=[pltpu.SemaphoreType.DMA((5 * ROWS,))],
        compiler_params=params(8),
    )(at, got.reshape(lines, model), *(pin(a) for a in (w_gate, w_up, far, down, *pieces)))
    act = call(middle_kernel, shape(3, lines, width), keep, lax.ppermute(send, "c", SWAP))
    sent = call(after_kernel, shape(lines, model), at, act, lax.ppermute(act, "c", SWAP), *weights, scalars=1)
    back = lax.all_to_all(sent.reshape(n_dp, CAP, model), DP, split_axis=0, concat_axis=0, tiled=True)
    mixed = call(
        combine_kernel,
        shape(ROWS, count_tok, 2 * cols),
        back.reshape(EXPERTS, copies, CAP, model), routes, gates,
    )
    mixed = lax.all_to_all(mixed, "y", split_axis=0, concat_axis=0, tiled=True)
    mixed = jnp.sum(mixed.astype(F32), axis=0).astype(BF16)
    return mixed[:, :cols], mixed[:, cols:]


def solution(mesh):
    size = dict(x=4, z=8, y=ROWS, c=2)
    fine = Mesh(mesh.devices.reshape(tuple(size.values())), tuple(size))
    dp, tensor = DP, ("y", "c")
    placed = (P(dp, None),) * 4 + (P(None, dp + tensor),) * 2 + (P(dp, tensor),)
    return jax.shard_map(
        body,
        mesh=fine,
        in_specs=placed,
        out_specs=(P(dp, tensor), P(dp, tensor)),
        check_vma=False,
    )
```

```python
import jax
import jax.numpy as jnp
from jax import lax
from jax.experimental import pallas as pl
from jax.experimental.pallas import tpu as pltpu
from jax.sharding import Mesh, PartitionSpec as P

EXPERTS = 8
CAP = 8
DP = ("x", "z")
SWAP = ((0, 1), (1, 0))
F32, BF16 = jnp.float32, jnp.bfloat16
VMEM = pl.BlockSpec(memory_space=pltpu.VMEM)
HBM = pl.BlockSpec(memory_space=pltpu.MemorySpace.HBM)
SMEM = pl.BlockSpec(memory_space=pltpu.SMEM)


def params(mib):
    return pltpu.CompilerParams(vmem_limit_bytes=mib * 2**20)


ROWS = 8
SHIFTS = (4, 3, 5, 2, 6, 1, 7)


def pin(a):
    return pltpu.with_memory_space_constraint(a, pltpu.MemorySpace.HBM)


def mm(a, b):
    return jnp.dot(a, b, preferred_element_type=F32)


def mm_t(a, b):
    return lax.dot_general(a, b, (((1,), (1,)), ((), ())), preferred_element_type=F32)


def shape(*dims, dtype=BF16):
    return jax.ShapeDtypeStruct(dims, dtype)


def slot_table(routes, gates, by_token):
    slots = EXPERTS * CAP
    count_tok = routes.shape[0] if by_token else routes.shape[1]
    dims, axis = ((count_tok, slots), 1) if by_token else ((slots, count_tok), 0)
    pick = (lambda a, k: a[:, k : k + 1]) if by_token else (lambda a, k: a[k : k + 1, :])
    slot = lax.broadcasted_iota(jnp.int32, dims, axis)
    first, second = pick(routes, 0) == slot // CAP, pick(routes, 1) == slot // CAP
    member = jnp.where(first | second, 1.0, 0.0).astype(BF16)
    a = lax.broadcasted_iota(jnp.int32, (count_tok, count_tok), axis)
    b = lax.broadcasted_iota(jnp.int32, (count_tok, count_tok), 1 - axis)
    earlier = jnp.where(a < b, 1.0, 0.0).astype(BF16)
    rank = mm(earlier, member) if by_token else mm(member, earlier)
    mine = jnp.where((rank == (slot % CAP).astype(F32)) & (first | second), 1.0, 0.0)
    gate = jnp.where(first, pick(gates, 0), 0.0) + jnp.where(second, pick(gates, 1), 0.0)
    return mine, mine * gate


def outbox_kernel(at_ref, tokens_hbm, cot_hbm, routes_hbm, gates_hbm, sent_ref, *rest):
    held, sems = rest[:4], rest[4]
    moves = zip((tokens_hbm, cot_hbm, routes_hbm, gates_hbm), held)
    copies = [pltpu.make_async_copy(*move, sems.at[i]) for i, move in enumerate(moves)]
    for copy in copies:
        copy.start()
    for copy in copies:
        copy.wait()
    tokens_ref, cot_ref, routes_ref, gates_ref = held
    model = tokens_ref.shape[1]
    half, cols = model // 2, model // ROWS // 2
    low = at_ref[0] == 0
    mine, gate = slot_table(routes_ref[...], gates_ref[...], False)
    gate = jnp.sum(gate, axis=1, keepdims=True)
    mine = mine.astype(BF16)

    def ours(ref):
        cut = [ref[:, i * cols : (i + 1) * cols] for i in range(2 * ROWS)]
        return jnp.concatenate([jnp.where(low, cut[2 * y], cut[2 * y + 1]) for y in range(ROWS)], axis=1)

    x = mm(mine, ours(tokens_ref)).reshape(EXPERTS, CAP, half).astype(BF16)
    dy = (mm(mine, ours(cot_ref)) * gate).reshape(EXPERTS, CAP, half).astype(BF16)
    for copy in range(sent_ref.shape[1]):
        sent_ref[:, copy, :, :half] = x
        sent_ref[:, copy, :, half:] = dy

def cut_kernel(at_ref, gate_hbm, up_hbm, down_hbm, *rest):
    cut, away_ref, sems = rest[: ROWS - 1], rest[ROWS - 1], rest[ROWS]
    cols, width = cut[0].shape
    moves = []
    for shift, to in zip(SHIFTS, cut):
        y = lax.rem(at_ref[1] + shift, ROWS)
        moves.append((down_hbm.at[:, pl.ds(pl.multiple_of(y * width, width), width)], to))
    for i, source in enumerate((gate_hbm, up_hbm)):
        for y in range(ROWS):
            rows = pl.ds(pl.multiple_of((2 * y + 1 - at_ref[0]) * cols, cols), cols)
            moves.append((source.at[rows], away_ref.at[i, pl.ds(y * cols, cols)]))
    copies = [pltpu.make_async_copy(*move, sems.at[i]) for i, move in enumerate(moves)]
    for copy in copies:
        copy.start()
    for copy in copies:
        copy.wait()


def weight_copies(at_ref, gate_hbm, up_hbm, far_hbm, down_hbm, pieces, gate_w, up_w, down_w, sems):
    cols, width = gate_w.shape[1], gate_w.shape[2] // 2
    steps = []
    for i, shift in enumerate((0, *SHIFTS)):
        y = lax.rem(at_ref[1] - shift + ROWS, ROWS)
        rows = pl.ds(pl.multiple_of((2 * y + at_ref[0]) * cols, cols), cols)
        far = pl.ds(pl.multiple_of(y * cols, cols), cols)
        own_units = pl.ds(pl.multiple_of(at_ref[1] * 2 * width, 2 * width), 2 * width)
        moves = [
            (gate_hbm.at[rows], gate_w.at[y, :, pl.ds(0, width)]),
            (far_hbm.at[0, far], gate_w.at[y, :, pl.ds(width, width)]),
            (up_hbm.at[rows], up_w.at[y, :, pl.ds(0, width)]),
            (far_hbm.at[1, far], up_w.at[y, :, pl.ds(width, width)]),
            (down_hbm.at[:, own_units] if shift == 0 else pieces[i - 1], down_w.at[y]),
        ]
        copies = [pltpu.make_async_copy(*move, sems.at[5 * i + j]) for j, move in enumerate(moves)]
        steps.append((y, copies))
    return steps


def before_kernel(at_ref, got_ref, gate_hbm, up_hbm, far_hbm, down_hbm, *rest):
    pieces, (part_ref, gate_w, up_w, down_w, sems) = rest[: ROWS - 1], rest[ROWS - 1 :]
    steps = weight_copies(at_ref, gate_hbm, up_hbm, far_hbm, down_hbm, pieces, gate_w, up_w, down_w, sems)
    for j in range(5):
        for _, copies in steps:
            copies[j].start()
    low = at_ref[0] == 0
    half = got_ref.shape[1] // 2
    width = part_ref.shape[2] // 2
    for i, (weight, part, needs) in enumerate(((gate_w, 0, (0, 1)), (up_w, 0, (2, 3)), (down_w, 1, (4,)))):
        for _, copies in steps:
            for j in needs:
                copies[j].wait()
        both = mm(got_ref[:, part * half : (part + 1) * half], weight[...].reshape(half, 2 * width))
        left, right = both[:, :width], both[:, width:]
        if part:
            left, right = jnp.where(low, left, right), jnp.where(low, right, left)
        part_ref[i, :, :width] = left
        part_ref[i, :, width:] = right


def activations(gate_pre, up_pre, d_hidden):
    s = jax.nn.sigmoid(gate_pre)
    activated = gate_pre * s
    return (
        (activated * up_pre).astype(BF16),
        (d_hidden * up_pre * s * (1.0 + gate_pre * (1.0 - s))).astype(BF16),
        (d_hidden * activated).astype(BF16),
    )


def after_kernel(at_ref, part_ref, came_ref, gate_w, up_w, down_w, sent_ref):
    low = at_ref[0] == 0
    block = 2 * gate_w.shape[1]
    width = part_ref.shape[2] // 2
    own = activations(*(part_ref[i, :, :width] + came_ref[i, :, width:] for i in range(3)))
    far = activations(*(part_ref[i, :, width:] + came_ref[i, :, :width] for i in range(3)))
    hidden = jnp.concatenate([jnp.where(low, own[0], far[0]), jnp.where(low, far[0], own[0])], axis=1)
    d_gate = jnp.concatenate([own[1], far[1]], axis=1)
    d_up = jnp.concatenate([own[2], far[2]], axis=1)
    for y in range(ROWS):
        out = mm_t(hidden, down_w[y])
        grad = mm_t(d_gate, gate_w[y]) + mm_t(d_up, up_w[y])
        sent_ref[:, y * block : (y + 1) * block] = jnp.concatenate([out, grad], axis=1).astype(BF16)


def combine_kernel(back_ref, routes_ref, gates_ref, mixed_ref):
    cols = mixed_ref.shape[2] // 2
    summed = back_ref[:, 0].astype(F32)
    for copy in range(1, back_ref.shape[1]):
        summed = summed + back_ref[:, copy].astype(F32)
    summed = summed.reshape(EXPERTS * CAP, -1)
    mine, gate = slot_table(routes_ref[...], gates_ref[...], True)

    def pick(weights, values):
        return jnp.dot(weights, values, precision=lax.Precision.HIGHEST, preferred_element_type=F32)

    for y in range(ROWS):
        out = pick(gate, summed[:, 2 * y * cols : (2 * y + 1) * cols])
        grad = pick(mine, summed[:, (2 * y + 1) * cols : 2 * (y + 1) * cols])
        mixed_ref[y] = jnp.concatenate([out, grad], axis=1).astype(BF16)


def call(kernel, out_shape, *args, scalars=0, mib=8):
    single = not isinstance(out_shape, list)
    return pl.pallas_call(
        kernel,
        in_specs=[SMEM] * scalars + [VMEM] * (len(args) - scalars),
        out_specs=VMEM if single else [VMEM] * len(out_shape),
        out_shape=out_shape,
        compiler_params=params(mib),
    )(*args)


def body(tokens, cotangent, routes, gates, w_gate, w_up, w_down):
    count_tok, model = tokens.shape
    n_dp = lax.axis_size(DP)
    copies = n_dp // EXPERTS
    cols, width = w_down.shape[1], w_gate.shape[1]
    lines, half = n_dp * CAP, model // 2
    at = jnp.stack([lax.axis_index("c"), lax.axis_index("y")]).astype(jnp.int32)
    down = w_down.T

    held = (tokens, cotangent, routes.T, gates.T)
    sent = pl.pallas_call(
        outbox_kernel,
        in_specs=[SMEM] + [HBM] * 4,
        out_specs=VMEM,
        out_shape=pltpu.VMEM((EXPERTS, copies, CAP, model), BF16),
        scratch_shapes=[pltpu.VMEM(a.shape, a.dtype) for a in held] + [pltpu.SemaphoreType.DMA((4,))],
        compiler_params=params(4),
    )(at, *(pin(a) for a in held))
    got = lax.all_to_all(sent.reshape(n_dp, CAP, model), DP, split_axis=0, concat_axis=0, tiled=True)

    *cut, away = pl.pallas_call(
        cut_kernel,
        in_specs=[SMEM] + [HBM] * 3,
        out_specs=[VMEM] * ROWS,
        out_shape=[pltpu.VMEM((cols, 2 * width), BF16)] * (ROWS - 1) + [pltpu.VMEM((2, half, width), BF16)],
        scratch_shapes=[pltpu.SemaphoreType.DMA((3 * ROWS - 1,))],
        compiler_params=params(1),
    )(at, pin(w_gate), pin(w_up), pin(down))
    far = lax.ppermute(away, "c", SWAP)
    *late, far = lax.optimization_barrier((*cut[4:], far))
    cut = (*cut[:4], *late)
    pieces = [lax.ppermute(a, "y", [(i, (i + s) % ROWS) for i in range(ROWS)]) for a, s in zip(cut, SHIFTS)]

    got, *pieces = lax.optimization_barrier((got, *pieces))
    part, *weights = pl.pallas_call(
        before_kernel,
        in_specs=[SMEM, VMEM] + [HBM] * (3 + ROWS),
        out_specs=[VMEM] * 4,
        out_shape=[shape(3, lines, 2 * width, dtype=F32)] + [shape(ROWS, cols, 2 * width)] * 3,
        scratch_shapes=[pltpu.SemaphoreType.DMA((5 * ROWS,))],
        compiler_params=params(8),
    )(at, got.reshape(lines, model), *(pin(a) for a in (w_gate, w_up, far, down, *pieces)))
    sent = call(after_kernel, shape(lines, model), at, part, lax.ppermute(part, "c", SWAP), *weights, scalars=1)
    back = lax.all_to_all(sent.reshape(n_dp, CAP, model), DP, split_axis=0, concat_axis=0, tiled=True)
    mixed = call(
        combine_kernel,
        shape(ROWS, count_tok, 2 * cols),
        back.reshape(EXPERTS, copies, CAP, model), routes, gates,
    )
    mixed = lax.all_to_all(mixed, "y", split_axis=0, concat_axis=0, tiled=True)
    mixed = jnp.sum(mixed.astype(F32), axis=0).astype(BF16)
    return mixed[:, :cols], mixed[:, cols:]


def solution(mesh):
    size = dict(x=4, z=8, y=ROWS, c=2)
    fine = Mesh(mesh.devices.reshape(tuple(size.values())), tuple(size))
    dp, tensor = DP, ("y", "c")
    placed = (P(dp, None),) * 4 + (P(None, dp + tensor),) * 2 + (P(dp, tensor),)
    return jax.shard_map(
        body,
        mesh=fine,
        in_specs=placed,
        out_specs=(P(dp, tensor), P(dp, tensor)),
        check_vma=False,
    )
```

```python
import jax
import jax.numpy as jnp
from jax import lax
from jax.experimental import pallas as pl
from jax.experimental.pallas import tpu as pltpu
from jax.sharding import Mesh, PartitionSpec as P

EXPERTS = 8
CAP = 8
DP = ("x", "z")
SWAP = ((0, 1), (1, 0))
F32, BF16 = jnp.float32, jnp.bfloat16
VMEM = pl.BlockSpec(memory_space=pltpu.VMEM)
HBM = pl.BlockSpec(memory_space=pltpu.MemorySpace.HBM)
SMEM = pl.BlockSpec(memory_space=pltpu.SMEM)


def params(mib):
    return pltpu.CompilerParams(vmem_limit_bytes=mib * 2**20)


ROWS = 8
SHIFTS = (4, 3, 5, 2, 6, 1, 7)


def pin(a):
    return pltpu.with_memory_space_constraint(a, pltpu.MemorySpace.HBM)


def mm(a, b):
    return jnp.dot(a, b, preferred_element_type=F32)


def mm_t(a, b):
    return lax.dot_general(a, b, (((1,), (1,)), ((), ())), preferred_element_type=F32)


def shape(*dims, dtype=BF16):
    return jax.ShapeDtypeStruct(dims, dtype)


def slot_table(routes, gates, by_token):
    slots = EXPERTS * CAP
    count_tok = routes.shape[0] if by_token else routes.shape[1]
    dims, axis = ((count_tok, slots), 1) if by_token else ((slots, count_tok), 0)
    pick = (lambda a, k: a[:, k : k + 1]) if by_token else (lambda a, k: a[k : k + 1, :])
    slot = lax.broadcasted_iota(jnp.int32, dims, axis)
    first, second = pick(routes, 0) == slot // CAP, pick(routes, 1) == slot // CAP
    member = jnp.where(first | second, 1.0, 0.0).astype(BF16)
    a = lax.broadcasted_iota(jnp.int32, (count_tok, count_tok), axis)
    b = lax.broadcasted_iota(jnp.int32, (count_tok, count_tok), 1 - axis)
    earlier = jnp.where(a < b, 1.0, 0.0).astype(BF16)
    rank = mm(earlier, member) if by_token else mm(member, earlier)
    mine = jnp.where((rank == (slot % CAP).astype(F32)) & (first | second), 1.0, 0.0)
    gate = jnp.where(first, pick(gates, 0), 0.0) + jnp.where(second, pick(gates, 1), 0.0)
    return mine, mine * gate


def outbox_kernel(at_ref, tokens_hbm, cot_hbm, routes_hbm, gates_hbm, sent_ref, *rest):
    held, sems = rest[:4], rest[4]
    moves = zip((tokens_hbm, cot_hbm, routes_hbm, gates_hbm), held)
    copies = [pltpu.make_async_copy(*move, sems.at[i]) for i, move in enumerate(moves)]
    for copy in copies:
        copy.start()
    for copy in copies:
        copy.wait()
    tokens_ref, cot_ref, routes_ref, gates_ref = held
    model = tokens_ref.shape[1]
    half, cols = model // 2, model // ROWS // 2
    low = at_ref[0] == 0
    mine, gate = slot_table(routes_ref[...], gates_ref[...], False)
    gate = jnp.sum(gate, axis=1, keepdims=True)
    mine = mine.astype(BF16)

    def ours(ref):
        cut = [ref[:, i * cols : (i + 1) * cols] for i in range(2 * ROWS)]
        return jnp.concatenate([jnp.where(low, cut[2 * y], cut[2 * y + 1]) for y in range(ROWS)], axis=1)

    x = mm(mine, ours(tokens_ref)).reshape(EXPERTS, CAP, half).astype(BF16)
    dy = (mm(mine, ours(cot_ref)) * gate).reshape(EXPERTS, CAP, half).astype(BF16)
    for copy in range(sent_ref.shape[1]):
        sent_ref[:, copy, :, :half] = x
        sent_ref[:, copy, :, half:] = dy

def cut_kernel(at_ref, gate_hbm, up_hbm, down_hbm, *rest):
    cut, away_ref, sems = rest[: ROWS - 1], rest[ROWS - 1], rest[ROWS]
    cols, width = cut[0].shape
    moves = []
    for shift, to in zip(SHIFTS, cut):
        y = lax.rem(at_ref[1] + shift, ROWS)
        moves.append((down_hbm.at[:, pl.ds(pl.multiple_of(y * width, width), width)], to))
    for i, source in enumerate((gate_hbm, up_hbm)):
        for y in range(ROWS):
            rows = pl.ds(pl.multiple_of((2 * y + 1 - at_ref[0]) * cols, cols), cols)
            moves.append((source.at[rows], away_ref.at[i, pl.ds(y * cols, cols)]))
    copies = [pltpu.make_async_copy(*move, sems.at[i]) for i, move in enumerate(moves)]
    for copy in copies:
        copy.start()
    for copy in copies:
        copy.wait()


def assemble_kernel(at_ref, gate_hbm, up_hbm, far_hbm, gate_w, up_w, sems):
    cols, width = gate_w.shape[1], gate_w.shape[2] // 2
    moves = []
    for i, (source, weight) in enumerate(((gate_hbm, gate_w), (up_hbm, up_w))):
        for y in range(ROWS):
            rows = pl.ds(pl.multiple_of((2 * y + at_ref[0]) * cols, cols), cols)
            moves.append((source.at[rows], weight.at[y, :, pl.ds(0, width)]))
            moves.append((far_hbm.at[i, pl.ds(y * cols, cols)], weight.at[y, :, pl.ds(width, width)]))
    copies = [pltpu.make_async_copy(*move, sems.at[i]) for i, move in enumerate(moves)]
    for copy in copies:
        copy.start()
    for copy in copies:
        copy.wait()


def before_kernel(at_ref, got_ref, gate_w, up_w, down_hbm, *rest):
    pieces, (part_ref, down_w, sems) = rest[: ROWS - 1], rest[ROWS - 1 :]
    width = part_ref.shape[2] // 2
    half = got_ref.shape[1] // 2
    own_units = pl.ds(pl.multiple_of(at_ref[1] * 2 * width, 2 * width), 2 * width)
    copies = []
    for i, (shift, piece) in enumerate(zip((0, *SHIFTS), (down_hbm.at[:, own_units], *pieces))):
        y = lax.rem(at_ref[1] - shift + ROWS, ROWS)
        copies.append(pltpu.make_async_copy(piece, down_w.at[y], sems.at[i]))
    for copy in copies:
        copy.start()
    for i, weight in enumerate((gate_w, up_w)):
        part_ref[i] = mm(got_ref[:, :half], weight[...].reshape(half, 2 * width))
    for copy in copies:
        copy.wait()
    both = mm(got_ref[:, half:], down_w[...].reshape(half, 2 * width))
    left, right = both[:, :width], both[:, width:]
    low = at_ref[0] == 0
    part_ref[2, :, :width] = jnp.where(low, left, right)
    part_ref[2, :, width:] = jnp.where(low, right, left)


def activations(gate_pre, up_pre, d_hidden):
    s = jax.nn.sigmoid(gate_pre)
    activated = gate_pre * s
    return (
        (activated * up_pre).astype(BF16),
        (d_hidden * up_pre * s * (1.0 + gate_pre * (1.0 - s))).astype(BF16),
        (d_hidden * activated).astype(BF16),
    )


def after_kernel(at_ref, part_ref, came_ref, gate_w, up_w, down_w, sent_ref):
    low = at_ref[0] == 0
    width = part_ref.shape[2] // 2
    own = activations(*(part_ref[i, :, :width] + came_ref[i, :, width:] for i in range(3)))
    far = activations(*(part_ref[i, :, width:] + came_ref[i, :, :width] for i in range(3)))
    hidden = jnp.concatenate([jnp.where(low, own[0], far[0]), jnp.where(low, far[0], own[0])], axis=1)
    d_gate = jnp.concatenate([own[1], far[1]], axis=1)
    d_up = jnp.concatenate([own[2], far[2]], axis=1)
    half = sent_ref.shape[1] // 2
    flat = lambda ref: ref[...].reshape(half, 2 * width)
    sent_ref[:, :half] = mm_t(hidden, flat(down_w)).astype(BF16)
    sent_ref[:, half:] = (mm_t(d_gate, flat(gate_w)) + mm_t(d_up, flat(up_w))).astype(BF16)


def combine_kernel(back_ref, routes_ref, gates_ref, mixed_ref):
    cols = mixed_ref.shape[2] // 2
    summed = back_ref[:, 0].astype(F32)
    for copy in range(1, back_ref.shape[1]):
        summed = summed + back_ref[:, copy].astype(F32)
    summed = summed.reshape(EXPERTS * CAP, -1)
    mine, gate = slot_table(routes_ref[...], gates_ref[...], True)

    def pick(weights, values):
        return jnp.dot(weights, values, precision=lax.Precision.HIGHEST, preferred_element_type=F32)

    half = ROWS * cols
    out, grad = pick(gate, summed[:, :half]), pick(mine, summed[:, half:])
    for y in range(ROWS):
        at = slice(y * cols, (y + 1) * cols)
        mixed_ref[y] = jnp.concatenate([out[:, at], grad[:, at]], axis=1).astype(BF16)


def call(kernel, out_shape, *args, scalars=0, mib=8):
    single = not isinstance(out_shape, list)
    return pl.pallas_call(
        kernel,
        in_specs=[SMEM] * scalars + [VMEM] * (len(args) - scalars),
        out_specs=VMEM if single else [VMEM] * len(out_shape),
        out_shape=out_shape,
        compiler_params=params(mib),
    )(*args)


def body(tokens, cotangent, routes, gates, w_gate, w_up, w_down):
    count_tok, model = tokens.shape
    n_dp = lax.axis_size(DP)
    copies = n_dp // EXPERTS
    cols, width = w_down.shape[1], w_gate.shape[1]
    lines, half = n_dp * CAP, model // 2
    at = jnp.stack([lax.axis_index("c"), lax.axis_index("y")]).astype(jnp.int32)
    down = w_down.T

    held = (tokens, cotangent, routes.T, gates.T)
    sent = pl.pallas_call(
        outbox_kernel,
        in_specs=[SMEM] + [HBM] * 4,
        out_specs=VMEM,
        out_shape=pltpu.VMEM((EXPERTS, copies, CAP, model), BF16),
        scratch_shapes=[pltpu.VMEM(a.shape, a.dtype) for a in held] + [pltpu.SemaphoreType.DMA((4,))],
        compiler_params=params(4),
    )(at, *(pin(a) for a in held))
    got = lax.all_to_all(sent.reshape(n_dp, CAP, model), DP, split_axis=0, concat_axis=0, tiled=True)

    *cut, away = pl.pallas_call(
        cut_kernel,
        in_specs=[SMEM] + [HBM] * 3,
        out_specs=[VMEM] * ROWS,
        out_shape=[pltpu.VMEM((cols, 2 * width), BF16)] * (ROWS - 1) + [pltpu.VMEM((2, half, width), BF16)],
        scratch_shapes=[pltpu.SemaphoreType.DMA((3 * ROWS - 1,))],
        compiler_params=params(1),
    )(at, pin(w_gate), pin(w_up), pin(down))
    far = lax.ppermute(away, "c", SWAP)
    *late, far = lax.optimization_barrier((*cut[4:], far))
    cut = (*cut[:4], *late)
    pieces = [lax.ppermute(a, "y", [(i, (i + s) % ROWS) for i in range(ROWS)]) for a, s in zip(cut, SHIFTS)]

    gate_all, up_all = pl.pallas_call(
        assemble_kernel,
        in_specs=[SMEM] + [HBM] * 3,
        out_specs=[VMEM] * 2,
        out_shape=[pltpu.VMEM((ROWS, cols, 2 * width), BF16)] * 2,
        scratch_shapes=[pltpu.SemaphoreType.DMA((4 * ROWS,))],
        compiler_params=params(1),
    )(at, pin(w_gate), pin(w_up), far)
    got, gate_all, up_all, *pieces = lax.optimization_barrier((got, gate_all, up_all, *pieces))
    part, down_all = pl.pallas_call(
        before_kernel,
        in_specs=[SMEM] + [VMEM] * 3 + [HBM] * ROWS,
        out_specs=[VMEM] * 2,
        out_shape=[shape(3, lines, 2 * width, dtype=F32), shape(ROWS, cols, 2 * width)],
        scratch_shapes=[pltpu.SemaphoreType.DMA((ROWS,))],
        compiler_params=params(4),
    )(at, got.reshape(lines, model), gate_all, up_all, *(pin(a) for a in (down, *pieces)))
    weights = (gate_all, up_all, down_all)
    sent = call(after_kernel, shape(lines, model), at, part, lax.ppermute(part, "c", SWAP), *weights, scalars=1)
    back = lax.all_to_all(sent.reshape(n_dp, CAP, model), DP, split_axis=0, concat_axis=0, tiled=True)
    mixed = call(
        combine_kernel,
        shape(ROWS, count_tok, 2 * cols),
        back.reshape(EXPERTS, copies, CAP, model), routes, gates,
    )
    mixed = lax.all_to_all(mixed, "y", split_axis=0, concat_axis=0, tiled=True)
    mixed = jnp.sum(mixed.astype(F32), axis=0).astype(BF16)
    return mixed[:, :cols], mixed[:, cols:]


def solution(mesh):
    size = dict(x=4, z=8, y=ROWS, c=2)
    fine = Mesh(mesh.devices.reshape(tuple(size.values())), tuple(size))
    dp, tensor = DP, ("y", "c")
    placed = (P(dp, None),) * 4 + (P(None, dp + tensor),) * 2 + (P(dp, tensor),)
    return jax.shard_map(
        body,
        mesh=fine,
        in_specs=placed,
        out_specs=(P(dp, tensor), P(dp, tensor)),
        check_vma=False,
    )
```

```python
import jax
import jax.numpy as jnp
from jax import lax
from jax.experimental import pallas as pl
from jax.experimental.pallas import tpu as pltpu
from jax.sharding import Mesh, PartitionSpec as P

EXPERTS = 8
CAP = 8
DP = ("x", "z")
SWAP = ((0, 1), (1, 0))
F32, BF16 = jnp.float32, jnp.bfloat16
VMEM = pl.BlockSpec(memory_space=pltpu.VMEM)
HBM = pl.BlockSpec(memory_space=pltpu.MemorySpace.HBM)
SMEM = pl.BlockSpec(memory_space=pltpu.SMEM)


def params(mib):
    return pltpu.CompilerParams(vmem_limit_bytes=mib * 2**20)


ROWS = 8
SHIFTS = (4, 3, 5, 2, 6, 1, 7)


def pin(a):
    return pltpu.with_memory_space_constraint(a, pltpu.MemorySpace.HBM)


def mm(a, b):
    return jnp.dot(a, b, preferred_element_type=F32)


def mm_t(a, b):
    return lax.dot_general(a, b, (((1,), (1,)), ((), ())), preferred_element_type=F32)


def shape(*dims, dtype=BF16):
    return jax.ShapeDtypeStruct(dims, dtype)


def slot_table(routes, gates, by_token):
    slots = EXPERTS * CAP
    count_tok = routes.shape[0] if by_token else routes.shape[1]
    dims, axis = ((count_tok, slots), 1) if by_token else ((slots, count_tok), 0)
    pick = (lambda a, k: a[:, k : k + 1]) if by_token else (lambda a, k: a[k : k + 1, :])
    slot = lax.broadcasted_iota(jnp.int32, dims, axis)
    first, second = pick(routes, 0) == slot // CAP, pick(routes, 1) == slot // CAP
    member = jnp.where(first | second, 1.0, 0.0).astype(BF16)
    a = lax.broadcasted_iota(jnp.int32, (count_tok, count_tok), axis)
    b = lax.broadcasted_iota(jnp.int32, (count_tok, count_tok), 1 - axis)
    earlier = jnp.where(a < b, 1.0, 0.0).astype(BF16)
    rank = mm(earlier, member) if by_token else mm(member, earlier)
    mine = jnp.where((rank == (slot % CAP).astype(F32)) & (first | second), 1.0, 0.0)
    gate = jnp.where(first, pick(gates, 0), 0.0) + jnp.where(second, pick(gates, 1), 0.0)
    return mine, mine * gate


def outbox_kernel(at_ref, tokens_hbm, cot_hbm, routes_hbm, gates_hbm, sent_ref, *rest):
    held, sems = rest[:4], rest[4]
    moves = zip((tokens_hbm, cot_hbm, routes_hbm, gates_hbm), held)
    copies = [pltpu.make_async_copy(*move, sems.at[i]) for i, move in enumerate(moves)]
    for copy in copies:
        copy.start()
    for copy in copies:
        copy.wait()
    tokens_ref, cot_ref, routes_ref, gates_ref = held
    model = tokens_ref.shape[1]
    half, cols = model // 2, model // ROWS // 2
    low = at_ref[0] == 0
    mine, gate = slot_table(routes_ref[...], gates_ref[...], False)
    gate = jnp.sum(gate, axis=1, keepdims=True)
    mine = mine.astype(BF16)

    def ours(ref):
        cut = [ref[:, i * cols : (i + 1) * cols] for i in range(2 * ROWS)]
        return jnp.concatenate([jnp.where(low, cut[2 * y], cut[2 * y + 1]) for y in range(ROWS)], axis=1)

    x = mm(mine, ours(tokens_ref)).reshape(EXPERTS, CAP, half).astype(BF16)
    dy = (mm(mine, ours(cot_ref)) * gate).reshape(EXPERTS, CAP, half).astype(BF16)
    for copy in range(sent_ref.shape[1]):
        sent_ref[:, copy, :, :half] = x
        sent_ref[:, copy, :, half:] = dy

def cut_kernel(at_ref, gate_hbm, up_hbm, down_hbm, *rest):
    cut, away_ref, sems = rest[: ROWS - 1], rest[ROWS - 1], rest[ROWS]
    cols, width = cut[0].shape
    moves = []
    for shift, to in zip(SHIFTS, cut):
        y = lax.rem(at_ref[1] + shift, ROWS)
        moves.append((down_hbm.at[:, pl.ds(pl.multiple_of(y * width, width), width)], to))
    for i, source in enumerate((gate_hbm, up_hbm)):
        for y in range(ROWS):
            rows = pl.ds(pl.multiple_of((2 * y + 1 - at_ref[0]) * cols, cols), cols)
            moves.append((source.at[rows], away_ref.at[i, pl.ds(y * cols, cols)]))
    copies = [pltpu.make_async_copy(*move, sems.at[i]) for i, move in enumerate(moves)]
    for copy in copies:
        copy.start()
    for copy in copies:
        copy.wait()


def assemble_kernel(at_ref, gate_hbm, up_hbm, far_hbm, gate_w, up_w, sems):
    cols, width = gate_w.shape[1], gate_w.shape[2] // 2
    moves = []
    for i, (source, weight) in enumerate(((gate_hbm, gate_w), (up_hbm, up_w))):
        for y in range(ROWS):
            rows = pl.ds(pl.multiple_of((2 * y + at_ref[0]) * cols, cols), cols)
            moves.append((source.at[rows], weight.at[y, :, pl.ds(0, width)]))
            moves.append((far_hbm.at[i, pl.ds(y * cols, cols)], weight.at[y, :, pl.ds(width, width)]))
    copies = [pltpu.make_async_copy(*move, sems.at[i]) for i, move in enumerate(moves)]
    for copy in copies:
        copy.start()
    for copy in copies:
        copy.wait()


def before_kernel(at_ref, got_hbm, gate_w, up_w, down_hbm, *rest):
    pieces, (part_ref, down_w, got_ref, sems) = rest[: ROWS - 1], rest[ROWS - 1 :]
    width = part_ref.shape[2] // 2
    half = got_ref.shape[1] // 2
    own_units = pl.ds(pl.multiple_of(at_ref[1] * 2 * width, 2 * width), 2 * width)
    halves = []
    for i in range(2):
        at = pl.ds(i * half, half)
        halves.append(pltpu.make_async_copy(got_hbm.at[:, at], got_ref.at[:, at], sems.at[ROWS + i]))
        halves[i].start()
    copies = []
    for i, (shift, piece) in enumerate(zip((0, *SHIFTS), (down_hbm.at[:, own_units], *pieces))):
        y = lax.rem(at_ref[1] - shift + ROWS, ROWS)
        copies.append(pltpu.make_async_copy(piece, down_w.at[y], sems.at[i]))
    for copy in copies:
        copy.start()
    halves[0].wait()
    for i, weight in enumerate((gate_w, up_w)):
        part_ref[i] = mm(got_ref[:, :half], weight[...].reshape(half, 2 * width))
    for copy in (halves[1], *copies):
        copy.wait()
    both = mm(got_ref[:, half:], down_w[...].reshape(half, 2 * width))
    left, right = both[:, :width], both[:, width:]
    low = at_ref[0] == 0
    part_ref[2, :, :width] = jnp.where(low, left, right)
    part_ref[2, :, width:] = jnp.where(low, right, left)


def activations(gate_pre, up_pre, d_hidden):
    s = jax.nn.sigmoid(gate_pre)
    activated = gate_pre * s
    return (
        (activated * up_pre).astype(BF16),
        (d_hidden * up_pre * s * (1.0 + gate_pre * (1.0 - s))).astype(BF16),
        (d_hidden * activated).astype(BF16),
    )


def after_kernel(at_ref, part_ref, came_ref, gate_w, up_w, down_w, sent_hbm, held, sems):
    low = at_ref[0] == 0
    width = part_ref.shape[2] // 2
    own = activations(*(part_ref[i, :, :width] + came_ref[i, :, width:] for i in range(3)))
    far = activations(*(part_ref[i, :, width:] + came_ref[i, :, :width] for i in range(3)))
    hidden = jnp.concatenate([jnp.where(low, own[0], far[0]), jnp.where(low, far[0], own[0])], axis=1)
    d_gate = jnp.concatenate([own[1], far[1]], axis=1)
    d_up = jnp.concatenate([own[2], far[2]], axis=1)
    half = held.shape[1] // 2
    flat = lambda ref: ref[...].reshape(half, 2 * width)
    copies = []
    for i in range(2):
        part = pl.ds(i * half, half)
        if i == 0:
            values = mm_t(hidden, flat(down_w))
        else:
            values = mm_t(d_gate, flat(gate_w)) + mm_t(d_up, flat(up_w))
        held[:, part] = values.astype(BF16)
        copies.append(pltpu.make_async_copy(held.at[:, part], sent_hbm.at[:, part], sems.at[i]))
        copies[i].start()
    for copy in copies:
        copy.wait()


def combine_kernel(back_ref, routes_ref, gates_ref, mixed_ref):
    cols = mixed_ref.shape[2] // 2
    summed = back_ref[:, 0].astype(F32)
    for copy in range(1, back_ref.shape[1]):
        summed = summed + back_ref[:, copy].astype(F32)
    summed = summed.reshape(EXPERTS * CAP, -1)
    mine, gate = slot_table(routes_ref[...], gates_ref[...], True)

    def pick(weights, values):
        return jnp.dot(weights, values, precision=lax.Precision.HIGHEST, preferred_element_type=F32)

    half = ROWS * cols
    out, grad = pick(gate, summed[:, :half]), pick(mine, summed[:, half:])
    for y in range(ROWS):
        at = slice(y * cols, (y + 1) * cols)
        mixed_ref[y] = jnp.concatenate([out[:, at], grad[:, at]], axis=1).astype(BF16)


def call(kernel, out_shape, *args, scalars=0, mib=8):
    single = not isinstance(out_shape, list)
    return pl.pallas_call(
        kernel,
        in_specs=[SMEM] * scalars + [VMEM] * (len(args) - scalars),
        out_specs=VMEM if single else [VMEM] * len(out_shape),
        out_shape=out_shape,
        compiler_params=params(mib),
    )(*args)


def body(tokens, cotangent, routes, gates, w_gate, w_up, w_down):
    count_tok, model = tokens.shape
    n_dp = lax.axis_size(DP)
    copies = n_dp // EXPERTS
    cols, width = w_down.shape[1], w_gate.shape[1]
    lines, half = n_dp * CAP, model // 2
    at = jnp.stack([lax.axis_index("c"), lax.axis_index("y")]).astype(jnp.int32)
    down = w_down.T

    held = (tokens, cotangent, routes.T, gates.T)
    sent = pl.pallas_call(
        outbox_kernel,
        in_specs=[SMEM] + [HBM] * 4,
        out_specs=VMEM,
        out_shape=pltpu.VMEM((EXPERTS, copies, CAP, model), BF16),
        scratch_shapes=[pltpu.VMEM(a.shape, a.dtype) for a in held] + [pltpu.SemaphoreType.DMA((4,))],
        compiler_params=params(4),
    )(at, *(pin(a) for a in held))
    got = lax.all_to_all(sent.reshape(n_dp, CAP, model), DP, split_axis=0, concat_axis=0, tiled=True)

    *cut, away = pl.pallas_call(
        cut_kernel,
        in_specs=[SMEM] + [HBM] * 3,
        out_specs=[VMEM] * ROWS,
        out_shape=[pltpu.VMEM((cols, 2 * width), BF16)] * (ROWS - 1) + [pltpu.VMEM((2, half, width), BF16)],
        scratch_shapes=[pltpu.SemaphoreType.DMA((3 * ROWS - 1,))],
        compiler_params=params(1),
    )(at, pin(w_gate), pin(w_up), pin(down))
    far = lax.ppermute(away, "c", SWAP)
    *late, far = lax.optimization_barrier((*cut[4:], far))
    cut = (*cut[:4], *late)
    pieces = [lax.ppermute(a, "y", [(i, (i + s) % ROWS) for i in range(ROWS)]) for a, s in zip(cut, SHIFTS)]

    gate_all, up_all = pl.pallas_call(
        assemble_kernel,
        in_specs=[SMEM] + [HBM] * 3,
        out_specs=[VMEM] * 2,
        out_shape=[pltpu.VMEM((ROWS, cols, 2 * width), BF16)] * 2,
        scratch_shapes=[pltpu.SemaphoreType.DMA((4 * ROWS,))],
        compiler_params=params(1),
    )(at, pin(w_gate), pin(w_up), far)
    got, gate_all, up_all, *pieces = lax.optimization_barrier((got, gate_all, up_all, *pieces))
    part, down_all = pl.pallas_call(
        before_kernel,
        in_specs=[SMEM, HBM] + [VMEM] * 2 + [HBM] * ROWS,
        out_specs=[VMEM] * 2,
        out_shape=[shape(3, lines, 2 * width, dtype=F32), shape(ROWS, cols, 2 * width)],
        scratch_shapes=[pltpu.VMEM((lines, model), BF16), pltpu.SemaphoreType.DMA((ROWS + 2,))],
        compiler_params=params(6),
    )(at, pin(got.reshape(lines, model)), gate_all, up_all, *(pin(a) for a in (down, *pieces)))
    weights = (gate_all, up_all, down_all)
    sent = pl.pallas_call(
        after_kernel,
        in_specs=[SMEM] + [VMEM] * 5,
        out_specs=HBM,
        out_shape=shape(lines, model),
        scratch_shapes=[pltpu.VMEM((lines, model), BF16), pltpu.SemaphoreType.DMA((2,))],
        compiler_params=params(10),
    )(at, part, lax.ppermute(part, "c", SWAP), *weights)
    back = lax.all_to_all(sent.reshape(n_dp, CAP, model), DP, split_axis=0, concat_axis=0, tiled=True)
    mixed = call(
        combine_kernel,
        shape(ROWS, count_tok, 2 * cols),
        back.reshape(EXPERTS, copies, CAP, model), routes, gates,
    )
    mixed = lax.all_to_all(mixed, "y", split_axis=0, concat_axis=0, tiled=True)
    mixed = jnp.sum(mixed.astype(F32), axis=0).astype(BF16)
    return mixed[:, :cols], mixed[:, cols:]


def solution(mesh):
    size = dict(x=4, z=8, y=ROWS, c=2)
    fine = Mesh(mesh.devices.reshape(tuple(size.values())), tuple(size))
    dp, tensor = DP, ("y", "c")
    placed = (P(dp, None),) * 4 + (P(None, dp + tensor),) * 2 + (P(dp, tensor),)
    return jax.shard_map(
        body,
        mesh=fine,
        in_specs=placed,
        out_specs=(P(dp, tensor), P(dp, tensor)),
        check_vma=False,
    )
```
